32 devices in a mesh: mem: 16 (over z, x, core), space: 2 (over y).
Axes of the slice: x: 2, y: 2, z: 4, core: 2. Of those that a mesh axis runs over, the one named last changes fastest.
Arguments:
- prior_samples: bfloat16 [256, 32, 4096], P('mem', 'space'), may hold values from -6 to 6
- diffusivity_field: float32 [32, 4096], P('space'), may hold values from 0.05 to 0.24
- measured_site_position: int32 [2, 16, 512], P('space', 'mem'), may hold values from 0 to 4095
- measured_quantities: float32 [2, 16, 512], P('space', 'mem'), may hold values from -6 to 6
- measurement_weightings: float32 [2, 16, 512], P('space', 'mem'), may hold values from 0.5 to 8
Outputs:
- analysis: bfloat16 [256, 32, 4096], P('mem', 'space')
The draws below stay inside these ranges and needn't reach their ends.
Inputs may be any that keep to these rules, and one draw needn't show every extreme that they name: measured_site_position[p, q, o] names cell a * 256 + b of patch (p, q) itself.
All inputs are finite; a program needn't handle non-finite values.
Results may differ from the reference program's by a relative error of at most 0.0077.
Values may be sent and summed in bfloat16 or wider, within the bound.
A program may use at most 64 MiB of HBM per device.

```python
import math
import jax
import jax.numpy as jnp
from jax import lax

SAMPLE_TOTAL = 256
A_DEV = 16
B_DEV = 256
OBS_DEV = 512
ITERS = 10
BLOCKS_A = 2
BLOCKS_B = 16
MESH_HEIGHT = 32
MESH_WIDTH = 4096


def with_ends(result, own_key, smallest, high):
    spot = [jax.random.randint(jax.random.fold_in(own_key, axis), (), 0, length) for axis, length in enumerate(result.shape)]
    longest = result.shape.index(max(result.shape))
    next_to = spot[:longest] + [(spot[longest] + 1) % result.shape[longest]] + spot[longest + 1:]
    return result.at[tuple(spot)].set(smallest).at[tuple(next_to)].set(high)


def steps_of(rng, dims, cuts, low, high):
    level, own = 1.0, jax.random.fold_in(rng, 6)
    for dim, shards_of in cuts:
        draws = jnp.exp(jax.random.uniform(jax.random.fold_in(own, dim), (shards_of,), jnp.float32, low / len(cuts), high / len(cuts)))
        level = level * jnp.repeat(draws, dims[dim] // shards_of).reshape([-1 if axis == dim else 1 for axis in range(len(dims))])
    return level


def scatter_about(stream_key, shape, scale, limit, split=(), kind=jnp.bfloat16):
    drawn = jax.random.normal(stream_key, shape, jnp.float32) * scale
    if len(split) > 0:
        drawn = steps_of(stream_key, shape, split, -0.22, 0.18) * drawn
    return jnp.clip(drawn, min=-limit, max=limit).astype(kind)


def setup_inputs(seed: int = 0) -> dict:
    arg_keys = jax.random.split(jax.random.key(seed), 6)
    prior_samples = scatter_about(arg_keys[0], (SAMPLE_TOTAL, MESH_HEIGHT, MESH_WIDTH), 1.0, 6.0, ((0, 16), (1, 2)))
    diffusivity_field = jnp.clip(0.05 + 0.19 * jax.random.uniform(arg_keys[1], (MESH_HEIGHT, MESH_WIDTH), jnp.float32) ** steps_of(arg_keys[1], (MESH_HEIGHT, MESH_WIDTH), ((0, 2),), -0.2, 0.2), 0.05, 0.24)
    measured_site_position = with_ends(jax.random.randint(arg_keys[2], (BLOCKS_A, BLOCKS_B, OBS_DEV), 0, A_DEV * B_DEV), jax.random.fold_in(arg_keys[2], 1), 0, (A_DEV * B_DEV) - 1).astype(jnp.int32)
    measured_quantities = scatter_about(arg_keys[3], (BLOCKS_A, BLOCKS_B, OBS_DEV), 1.0, 6.0, ((0, 2), (1, 16)), jnp.float32)
    measurement_weightings = jnp.clip(jnp.exp(math.log(8.0) - 2.7725887 * jax.random.uniform(arg_keys[4], (BLOCKS_A, BLOCKS_B, OBS_DEV), jnp.float32) ** steps_of(arg_keys[4], (BLOCKS_A, BLOCKS_B, OBS_DEV), ((0, 2), (1, 16)), -0.2, 0.2)), 0.5, 8.0)
    return {"prior_samples": prior_samples, "diffusivity_field": diffusivity_field, "measured_site_position": measured_site_position, "measured_quantities": measured_quantities, "measurement_weightings": measurement_weightings}


LOCALITY = ((0.25, 0.5, 0.25), (0.5, 1.0, 0.5), (0.25, 0.5, 0.25))
HIGHEST = lax.Precision.HIGHEST

def laplace(grid):
    padded = jnp.pad(grid, ((1, 1), (1, 1)))
    return padded[2:, 1:-1] + padded[:-2, 1:-1] + padded[1:-1, 2:] + padded[1:-1, :-2] - 4.0 * grid

def advance_prior(sample_label, diffusivity_field):
    present_sample = sample_label.astype(jnp.float32)
    present_sample = present_sample + diffusivity_field * laplace(present_sample)
    present_sample = present_sample + diffusivity_field * laplace(present_sample)
    return present_sample.astype(jnp.bfloat16)

def finish(sample_label, diffusivity_field):
    present_sample = sample_label.astype(jnp.float32)
    return (present_sample + diffusivity_field * laplace(present_sample)).astype(jnp.bfloat16)

def observe(patch_cells, indices, values, obs_weight):
    observed = jnp.take(patch_cells, indices, axis=1).astype(jnp.float32)
    obs_mean = lax.optimization_barrier(jnp.mean(observed, axis=0))
    obs_root = jnp.sqrt(obs_weight)
    spread = ((observed - obs_mean[None, :]) * obs_root[None, :]).astype(jnp.bfloat16)
    innovation = ((values - obs_mean) * obs_root).astype(jnp.bfloat16)
    spread_full = spread.astype(jnp.float32)
    own_gram = jnp.dot(spread_full, spread_full.T, precision=HIGHEST)
    own_vector = jnp.dot(spread_full, innovation.astype(jnp.float32), precision=HIGHEST)
    return (own_gram, own_vector)

def analyse(patch_cells, gram, vector):
    identity = jnp.eye(SAMPLE_TOTAL, dtype=jnp.float32)
    system = gram + (SAMPLE_TOTAL - 1.0) * identity
    frobenius = jnp.sqrt(jnp.sum(system * system))

    def newton(counter, pair):
        root_part, inverse_part = pair
        factor = 1.5 * identity - 0.5 * jnp.dot(inverse_part, root_part, precision=HIGHEST)
        return (jnp.dot(root_part, factor, precision=HIGHEST), jnp.dot(factor, inverse_part, precision=HIGHEST))
    root_part, inverse_part = lax.fori_loop(0, ITERS, newton, (system / frobenius, identity))
    inverse_root = inverse_part / jnp.sqrt(frobenius)
    mean_weights = jnp.dot(inverse_root, jnp.dot(inverse_root, vector, precision=HIGHEST), precision=HIGHEST)
    transform = (jnp.sqrt(SAMPLE_TOTAL - 1.0) * inverse_root + mean_weights[:, None]).astype(jnp.bfloat16)
    cells_full = patch_cells.astype(jnp.float32)
    state_mean = lax.optimization_barrier(jnp.mean(cells_full, axis=0))
    deviation = (cells_full - state_mean[None, :]).astype(jnp.bfloat16)
    moved = jnp.dot(transform.astype(jnp.float32).T, deviation.astype(jnp.float32), precision=HIGHEST)
    return (state_mean[None, :] + moved).astype(jnp.bfloat16)

def reference(prior_samples, diffusivity_field, measured_site_position, measured_quantities, measurement_weightings):
    advanced_sample = lax.map(lambda sample_label: advance_prior(sample_label, diffusivity_field), prior_samples)
    patches = advanced_sample.reshape(SAMPLE_TOTAL, BLOCKS_A, A_DEV, BLOCKS_B, B_DEV).transpose(1, 3, 0, 2, 4)
    patches = patches.reshape(BLOCKS_A, BLOCKS_B, SAMPLE_TOTAL, A_DEV * B_DEV)
    own_grams, own_vectors = lax.map(lambda group: jax.vmap(observe)(*group), (patches, measured_site_position, measured_quantities, measurement_weightings))
    padded_grams = jnp.pad(own_grams, ((1, 1), (1, 1), (0, 0), (0, 0)))
    padded_vectors = jnp.pad(own_vectors, ((1, 1), (1, 1), (0, 0)))
    gram = jnp.zeros_like(own_grams)
    vector = jnp.zeros_like(own_vectors)
    for first in range(3):
        for second in range(3):
            gram = gram + LOCALITY[first][second] * padded_grams[first:first + BLOCKS_A, second:second + BLOCKS_B]
            vector = vector + LOCALITY[first][second] * padded_vectors[first:first + BLOCKS_A, second:second + BLOCKS_B]
    updated = lax.map(lambda group: jax.vmap(analyse)(*group), (patches, gram, vector))
    updated = updated.reshape(BLOCKS_A, BLOCKS_B, SAMPLE_TOTAL, A_DEV, B_DEV).transpose(2, 0, 3, 1, 4).reshape(SAMPLE_TOTAL, MESH_HEIGHT, MESH_WIDTH)
    return lax.map(lambda sample_label: finish(sample_label, diffusivity_field), updated)
```

```python
import functools
import math

import jax
import jax.numpy as jnp
from jax import lax
from jax.experimental import pallas as pl
from jax.experimental.pallas import tpu as pltpu
from jax.sharding import PartitionSpec as P

ITERS = 10
PAD = 128
F32 = jnp.float32
BF16 = jnp.bfloat16
VMEM = pl.BlockSpec(memory_space=pltpu.VMEM)


def exchange(low_edge, high_edge, axis):
    count = lax.axis_size(axis)
    forward = [(i, i + 1) for i in range(count - 1)]
    backward = [(target, source) for source, target in forward]
    return lax.ppermute(high_edge, axis, forward), lax.ppermute(low_edge, axis, backward)


def swap_matrix(outer, inner):
    size = outer * inner
    row = lax.broadcasted_iota(jnp.int32, (size, size), 0)
    col = lax.broadcasted_iota(jnp.int32, (size, size), 1)
    return ((row % inner) * outer + row // inner == col).astype(BF16)


def merged(block):
    a, m, c = block.shape
    if m % 16 == 0:
        return block.reshape(a * m, c)
    return block.astype(F32).reshape(a * m, c).astype(BF16)


def halves(value):
    high = value.astype(BF16)
    return high, (value - high.astype(F32)).astype(BF16)


def dot1(a, b):
    return jnp.dot(a, b, preferred_element_type=F32)


def dot3(a, b):
    ah, al = a
    bh, bl = b
    return dot1(ah, bh) + (dot1(ah, bl) + dot1(al, bh))


def step_row(src, row, diffusion, width):
    mid = src[row, :, PAD : PAD + width]
    around = (
        src[row - 1, :, PAD : PAD + width]
        + src[row + 1, :, PAD : PAD + width]
        + src[row, :, PAD - 1 : PAD - 1 + width]
        + src[row, :, PAD + 1 : PAD + 1 + width]
    )
    return mid + diffusion * (around - 4.0 * mid)


def clear_pads(buf, width):
    rows, m, _ = buf.shape
    buf[:, :, :PAD] = jnp.zeros((rows, m, PAD), F32)
    buf[:, :, PAD + width :] = jnp.zeros((rows, m, PAD), F32)


def forecast_kernel(x_ref, swap_ref, d_ref, low_ref, high_ref, out_ref, xs, v1):
    patches, rows, m, cols = out_ref.shape
    width = patches * cols
    clear_pads(xs, width)
    clear_pads(v1, width)
    xs[0:2, :, PAD : PAD + width] = low_ref[...].astype(F32)
    xs[rows + 2 : rows + 4, :, PAD : PAD + width] = high_ref[...].astype(F32)

    @pl.loop(0, patches // 2)
    def _(c):
        at = pl.multiple_of(c * 2 * cols, 128)
        part = dot1(swap_ref[...], x_ref[:, pl.ds(at, 2 * cols)])
        xs[2 : rows + 2, :, pl.ds(at + PAD, 2 * cols)] = part.reshape(rows, m, 2 * cols)

    @pl.loop(1, rows + 3)
    def _(r):
        v1[r, :, PAD : PAD + width] = step_row(xs, r, d_ref[r - 1], width)

    @pl.loop(2, rows + 2)
    def _(r):
        fresh = step_row(v1, r, d_ref[r - 1], width).astype(BF16)
        for q in range(patches):
            out_ref[q, r - 2] = fresh[:, q * cols : (q + 1) * cols]


def observe_kernel(patch_ref, site_ref, value_ref, weight_ref, out_ref, acc):
    owners, rows, m, cols = patch_ref.shape
    members = owners * m
    obs = site_ref.shape[1]
    acc[...] = jnp.zeros_like(acc)

    @pl.loop(0, rows)
    def _(r):
        cell = lax.broadcasted_iota(jnp.int32, (cols, obs), 0) + r * cols
        picked = jnp.where(cell == site_ref[...], 1.0, 0.0).astype(BF16)
        acc[...] += dot1(merged(patch_ref[:, r]), picked)

    observed = acc[...]
    obs_mean = jnp.sum(observed, axis=0, keepdims=True) * (1.0 / members)
    root = jnp.sqrt(weight_ref[...])
    spread = ((observed - obs_mean) * root).astype(BF16)
    innovation = ((value_ref[...] - obs_mean) * root).astype(BF16)
    contract = (((1,), (1,)), ((), ()))
    out_ref[0:members, :] = lax.dot_general(spread, spread, contract, preferred_element_type=F32)
    wide = jnp.broadcast_to(innovation.astype(F32), (8, obs)).astype(BF16)
    out_ref[members : members + 8, :] = lax.dot_general(
        wide, spread, contract, preferred_element_type=F32
    )


def analyse_kernel(gram_ref, patch_ref, out_ref):
    owners, rows, m, cols = patch_ref.shape
    members = owners * m
    identity = (
        lax.broadcasted_iota(jnp.int32, (members, members), 0)
        == lax.broadcasted_iota(jnp.int32, (members, members), 1)
    ).astype(F32)
    system = gram_ref[0:members, :] + (members - 1.0) * identity
    vector = gram_ref[members : members + 8, :]
    frob = jnp.sqrt(jnp.sum(jnp.sum(system * system, axis=1, keepdims=True), axis=0, keepdims=True))
    root_part = system / frob
    factor = 1.5 * identity - 0.5 * root_part
    root_part = dot3(halves(root_part), halves(factor))
    inverse_part = factor
    for step in range(1, ITERS):
        r, z = halves(root_part), halves(inverse_part)
        f = halves(1.5 * identity - 0.5 * dot3(z, r))
        if step < ITERS - 1:
            root_part = dot3(r, f)
        inverse_part = dot3(f, z)
    inverse_root = inverse_part / jnp.sqrt(frob)
    z = halves(inverse_root)
    weights = dot3(halves(dot3(halves(vector), z)), z)[0:1, :]
    turned = (math.sqrt(members - 1.0) * inverse_root + weights).astype(BF16)

    @pl.loop(0, rows)
    def _(r):
        cells = merged(patch_ref[:, r]).astype(F32)
        mean = jnp.sum(cells, axis=0, keepdims=True) * (1.0 / members)
        updated = mean + dot1(turned, (cells - mean).astype(BF16))
        out_ref[:, r] = updated.reshape(owners, m, cols).astype(BF16)


def finish_kernel(x_ref, swap_ref, d_ref, low_ref, high_ref, out_ref, xs, moved):
    patches, rows, m, cols = x_ref.shape
    width = patches * cols
    clear_pads(xs, width)
    for q in range(patches):
        at = slice(PAD + q * cols, PAD + (q + 1) * cols)
        xs[0, :, at] = low_ref[q].astype(F32)
        xs[rows + 1, :, at] = high_ref[q].astype(F32)
        xs[1 : rows + 1, :, at] = x_ref[q].astype(F32)

    @pl.loop(1, rows + 1)
    def _(r):
        moved[r - 1] = step_row(xs, r, d_ref[r - 1], width).astype(BF16)

    @pl.loop(0, patches // 2)
    def _(c):
        at = pl.multiple_of(c * 2 * cols, 128)
        part = merged(moved[:, :, pl.ds(at, 2 * cols)])
        out_ref[:, pl.ds(at, 2 * cols)] = dot1(swap_ref[...], part).astype(BF16)


def call(kernel, out_shape, out_dtype, scratch, *args, name, flops):
    size = sum(a.size * a.dtype.itemsize for a in args)
    return pl.pallas_call(
        kernel,
        out_shape=jax.ShapeDtypeStruct(out_shape, out_dtype),
        in_specs=[VMEM] * len(args),
        out_specs=VMEM,
        scratch_shapes=scratch,
        compiler_params=pltpu.CompilerParams(vmem_limit_bytes=50 * 2**20),
        cost_estimate=pl.CostEstimate(flops=flops, bytes_accessed=size, transcendentals=0),
        name=name,
    )(*args)


def body(prior, diffusivity, site, quantities, weightings):
    m, rows, width = prior.shape
    patches = lax.axis_size("mem")
    cols = width // patches
    members = m * patches
    obs = site.shape[-1]

    def edge(two_rows, one_row):
        high, low = halves(one_row)
        return jnp.concatenate(
            [jnp.transpose(two_rows, (1, 0, 2)).reshape(2 * m, width), high, low], axis=0
        )

    low, high = exchange(
        edge(prior[:, :2], diffusivity[:1]), edge(prior[:, -2:], diffusivity[-1:]), "space"
    )

    def split(got):
        return (
            got[: 2 * m].reshape(2, m, width),
            got[2 * m : 2 * m + 1].astype(F32) + got[2 * m + 1 :].astype(F32),
        )

    (low_x, low_d), (high_x, high_d) = split(low), split(high)
    d_ext = jnp.concatenate([low_d, diffusivity, high_d], axis=0)[:, None, :]
    padded = width + 2 * PAD
    fresh = call(
        forecast_kernel,
        (patches, rows, m, cols),
        BF16,
        [pltpu.VMEM((rows + 4, m, padded), F32), pltpu.VMEM((rows + 4, m, padded), F32)],
        prior.reshape(m * rows, width),
        swap_matrix(rows, m),
        d_ext,
        low_x,
        high_x,
        name="forecast",
        flops=2 * (m * rows) ** 2 * width,
    )
    patch = lax.all_to_all(fresh, "mem", split_axis=0, concat_axis=0, tiled=True)
    own = call(
        observe_kernel,
        (members + 8, members),
        F32,
        [pltpu.VMEM((members, obs), F32)],
        patch,
        site[0],
        quantities[0],
        weightings[0],
        name="observe",
        flops=2 * members * obs * (rows * cols + members),
    )
    sent = own.astype(BF16)
    low, high = exchange(sent, sent, "mem")
    band = own + 0.5 * (low.astype(F32) + high.astype(F32))
    sent = band.astype(BF16)
    low, high = exchange(sent, sent, "space")
    gram = band + 0.5 * (low.astype(F32) + high.astype(F32))
    updated = call(
        analyse_kernel,
        (patches, rows, m, cols),
        BF16,
        [],
        gram,
        patch,
        name="analyse",
        flops=2 * members * members * (rows * cols + 90 * members),
    )
    back = lax.all_to_all(updated, "mem", split_axis=0, concat_axis=0, tiled=True)
    low, high = exchange(back[:, 0], back[:, -1], "space")
    out = call(
        finish_kernel,
        (m * rows, width),
        BF16,
        [pltpu.VMEM((rows + 2, m, padded), F32), pltpu.VMEM((rows, m, width), BF16)],
        back,
        swap_matrix(m, rows),
        diffusivity[:, None, :],
        low,
        high,
        name="finish",
        flops=2 * (m * rows) ** 2 * width,
    )
    return out.reshape(m, rows, width)


def solution(mesh):
    return jax.shard_map(
        body,
        mesh=mesh,
        in_specs=(
            P("mem", "space", None),
            P("space", None),
            P("space", "mem", None),
            P("space", "mem", None),
            P("space", "mem", None),
        ),
        out_specs=P("mem", "space", None),
        check_vma=False,
    )
```

```python
import functools
import math

import jax
import jax.numpy as jnp
from jax import lax
from jax.experimental import pallas as pl
from jax.experimental.pallas import tpu as pltpu
from jax.sharding import PartitionSpec as P

ITERS = 10
PAD = 128
F32 = jnp.float32
BF16 = jnp.bfloat16
MESH = pl.DeviceIdType.MESH
VMEM = pl.BlockSpec(memory_space=pltpu.VMEM)


def exchange(low_edge, high_edge, axis):
    count = lax.axis_size(axis)
    forward = [(i, i + 1) for i in range(count - 1)]
    backward = [(target, source) for source, target in forward]
    return lax.ppermute(high_edge, axis, forward), lax.ppermute(low_edge, axis, backward)


def swap_matrix(outer, inner):
    size = outer * inner
    row = lax.broadcasted_iota(jnp.int32, (size, size), 0)
    col = lax.broadcasted_iota(jnp.int32, (size, size), 1)
    return ((row % inner) * outer + row // inner == col).astype(BF16)


def merged(block):
    a, m, c = block.shape
    if m % 16 == 0:
        return block.reshape(a * m, c)
    return block.astype(F32).reshape(a * m, c).astype(BF16)


def halves(value):
    high = value.astype(BF16)
    return high, (value - high.astype(F32)).astype(BF16)


def dot1(a, b):
    return jnp.dot(a, b, preferred_element_type=F32)


def dot3(a, b):
    ah, al = a
    bh, bl = b
    return dot1(ah, bh) + (dot1(ah, bl) + dot1(al, bh))


def step(src, row, diffusion, at, cols):
    lo = PAD + at
    mid = src[row, :, lo : lo + cols]
    around = (
        src[row - 1, :, lo : lo + cols]
        + src[row + 1, :, lo : lo + cols]
        + src[row, :, lo - 1 : lo - 1 + cols]
        + src[row, :, lo + 1 : lo + 1 + cols]
    )
    return mid + diffusion * (around - 4.0 * mid)


def clear_pads(buf, width):
    rows, m, _ = buf.shape
    buf[:, :, :PAD] = jnp.zeros((rows, m, PAD), F32)
    buf[:, :, PAD + width :] = jnp.zeros((rows, m, PAD), F32)


class Peers:
    def __init__(self, n, spaces):
        self.n = n
        self.me = lax.axis_index("mem")
        self.space = lax.axis_index("space")
        self.has_low = self.space > 0
        self.has_high = self.space < spaces - 1
        self.order = []
        for k in reversed(range(1, n)):
            peer, bit = self.me, 1
            while bit < n:
                if k & bit:
                    peer = peer + bit * (1 - 2 * ((self.me // bit) % 2))
                bit *= 2
            self.order.append(peer)

    def sides(self):
        return ((self.has_low, self.space - 1), (self.has_high, self.space + 1))

    def greet(self):
        barrier = pltpu.get_barrier_semaphore()
        for peer in self.order:
            pl.semaphore_signal(barrier, inc=1, device_id={"mem": peer}, device_id_type=MESH)
        for has, other in self.sides():

            @pl.when(has)
            def _():
                pl.semaphore_signal(barrier, inc=1, device_id={"space": other}, device_id_type=MESH)

    def meet(self):
        barrier = pltpu.get_barrier_semaphore()
        beside = self.has_low.astype(jnp.int32) + self.has_high.astype(jnp.int32)
        pl.semaphore_wait(barrier, self.n - 1 + beside)


class Blocks:
    def __init__(self, peers, src, dst, groups, send, recv):
        self.peers, self.src, self.dst = peers, src, dst
        self.groups, self.sems = groups, (send, recv)

    def copy(self, g, i, slot):
        first, last = self.groups[g]
        peer = self.peers.order[i]
        send, recv = self.sems
        return pltpu.make_async_remote_copy(
            src_ref=self.src.at[peer, first:last],
            dst_ref=self.dst.at[slot, first:last],
            send_sem=send.at[g, i],
            recv_sem=recv.at[g, i],
            device_id={"mem": peer},
            device_id_type=MESH,
        )

    def start(self, g):
        for i in range(len(self.peers.order)):
            self.copy(g, i, self.peers.me).start()
        first, last = self.groups[g]
        me = self.peers.me
        self.dst[me, first:last] = self.src[me, first:last]

    def arrive(self, g):
        for i in range(len(self.peers.order)):
            self.copy(g, i, self.peers.order[i]).wait_recv()

    def finish(self):
        for g in range(len(self.groups)):
            for i in range(len(self.peers.order)):
                self.copy(g, i, self.peers.me).wait_send()


def beside(src, dst, sems, slot, other):
    send, recv = sems
    return pltpu.make_async_remote_copy(
        src_ref=src,
        dst_ref=dst,
        send_sem=send.at[slot],
        recv_sem=recv.at[slot],
        device_id={"space": other},
        device_id_type=MESH,
    )


def cut(first, last, parts):
    size = -(-(last - first) // parts)
    return [(a, min(a + size, last)) for a in range(first, last, size)]


def forecast_groups(rows):
    return cut(2, rows - 2, 3) + [(0, 2), (rows - 2, rows)]


def forecast_kernel(
    spaces, x_ref, swap_ref, d_ref, site_ref, value_ref, weight_ref, patch_ref, gram_ref,
    xs, v1, fresh, edge_out, edge_in, d_in, acc, send, recv, side_send, side_recv,
):
    patches, rows, m, cols = patch_ref.shape
    width = patches * cols
    members = patches * m
    obs = site_ref.shape[1]
    peers = Peers(patches, spaces)
    peers.greet()
    groups = forecast_groups(rows)
    blocks = Blocks(peers, fresh, patch_ref, groups, send, recv)
    clear_pads(xs, width)
    clear_pads(v1, width)

    for c in range(patches // 2):
        at = c * 2 * cols
        part = dot1(swap_ref[...], x_ref[:, at : at + 2 * cols]).reshape(rows, m, 2 * cols)
        xs[2 : rows + 2, :, PAD + at : PAD + at + 2 * cols] = part
        edge_out[0, :, :, at : at + 2 * cols] = part[:2].astype(BF16)
        edge_out[1, :, :, at : at + 2 * cols] = part[rows - 2 :].astype(BF16)

    peers.meet()
    side = (side_send, side_recv)

    def halo(k, other):
        return (
            beside(edge_out.at[k], edge_in.at[1 - k], side, k, other),
            beside(d_ref.at[0 if k == 0 else rows - 1], d_in.at[1 - k], side, 2 + k, other),
        )

    def halo_in(k, other):
        return (
            beside(edge_out.at[k], edge_in.at[k], side, 1 - k, other),
            beside(d_ref.at[0], d_in.at[k], side, 3 - k, other),
        )

    for k, (has, other) in enumerate(peers.sides()):

        @pl.when(has)
        def _():
            for copy in halo(k, other):
                copy.start()

    def first_step(r, d_row):
        for q in range(patches):
            at = q * cols
            v1[r, :, PAD + at : PAD + at + cols] = step(xs, r, d_row(at), at, cols)

    def second_step(r):
        for q in range(patches):
            at = q * cols
            fresh[q, r - 2] = step(v1, r, d_ref[r - 2, :, at : at + cols], at, cols).astype(BF16)

    done = 3
    for g in range(len(groups) - 2):
        first, last = groups[g]

        @pl.loop(done, last + 3)
        def _(r):
            first_step(r, lambda at: d_ref[r - 2, :, at : at + cols])

        done = last + 3

        @pl.loop(first + 2, last + 2)
        def _(r):
            second_step(r)

        blocks.start(g)

    for k, (has, other) in enumerate(peers.sides()):
        row = 0 if k == 0 else rows + 2

        @pl.when(has)
        def _():
            for copy in halo_in(k, other):
                copy.wait_recv()
            xs[row : row + 2, :, PAD : PAD + width] = edge_in[k].astype(F32)

        @pl.when(jnp.logical_not(has))
        def _():
            xs[row : row + 2, :, PAD : PAD + width] = jnp.zeros((2, m, width), F32)
            d_in[k] = jnp.zeros((1, width), F32)

    for k in range(2):
        outer, inner = (1, 2) if k == 0 else (rows + 2, rows + 1)
        first_step(outer, lambda at: d_in[k, :, at : at + cols])
        first_step(inner, lambda at: d_ref[inner - 2, :, at : at + cols])
        g = len(groups) - 2 + k

        @pl.loop(groups[g][0] + 2, groups[g][1] + 2)
        def _(r):
            second_step(r)

        blocks.start(g)

    acc[...] = jnp.zeros_like(acc)
    for g, (first, last) in enumerate(groups):
        blocks.arrive(g)

        @pl.loop(first, last)
        def _(r):
            cell = lax.broadcasted_iota(jnp.int32, (cols, obs), 0) + r * cols
            picked = jnp.where(cell == site_ref[...], 1.0, 0.0).astype(BF16)
            acc[...] += dot1(merged(patch_ref[:, r]), picked)

    observed = acc[...]
    obs_mean = jnp.sum(observed, axis=0, keepdims=True) * (1.0 / members)
    root = jnp.sqrt(weight_ref[...])
    spread = ((observed - obs_mean) * root).astype(BF16)
    innovation = ((value_ref[...] - obs_mean) * root).astype(BF16)
    contract = (((1,), (1,)), ((), ()))
    gram_ref[0:members, :] = lax.dot_general(spread, spread, contract, preferred_element_type=F32)
    wide = jnp.broadcast_to(innovation.astype(F32), (8, obs)).astype(BF16)
    gram_ref[members : members + 8, :] = lax.dot_general(
        wide, spread, contract, preferred_element_type=F32
    )
    blocks.finish()
    for k, (has, other) in enumerate(peers.sides()):

        @pl.when(has)
        def _():
            for copy in halo(k, other):
                copy.wait_send()


def transform_of(gram, vector, members):
    identity = (
        lax.broadcasted_iota(jnp.int32, (members, members), 0)
        == lax.broadcasted_iota(jnp.int32, (members, members), 1)
    ).astype(F32)
    system = gram + (members - 1.0) * identity
    frob = jnp.sqrt(jnp.sum(jnp.sum(system * system, axis=1, keepdims=True), axis=0, keepdims=True))
    root_part = system / frob
    factor = 1.5 * identity - 0.5 * root_part
    root_part = dot3(halves(root_part), halves(factor))
    inverse_part = factor
    for index in range(1, ITERS):
        r, z = halves(root_part), halves(inverse_part)
        f = halves(1.5 * identity - 0.5 * dot3(z, r))
        if index < ITERS - 1:
            root_part = dot3(r, f)
        inverse_part = dot3(f, z)
    inverse_root = inverse_part / jnp.sqrt(frob)
    z = halves(inverse_root)
    weights = dot3(halves(dot3(halves(vector), z)), z)[0:1, :]
    return (math.sqrt(members - 1.0) * inverse_root + weights).astype(BF16)


def analyse_groups(rows):
    return [(0, 1), (rows - 1, rows)] + cut(1, rows - 1, 3)


def analyse_kernel(
    spaces, gram_ref, patch_ref, swap_ref, d_ref, out_ref,
    updated, back, edge_in, turned, xs, moved, send, recv, side_send, side_recv,
):
    patches, rows, m, cols = patch_ref.shape
    width = patches * cols
    members = patches * m
    peers = Peers(patches, spaces)
    peers.greet()
    groups = analyse_groups(rows)
    blocks = Blocks(peers, updated, back, groups, send, recv)
    clear_pads(xs, width)
    turned[...] = transform_of(gram_ref[0:members, :], gram_ref[members:, :], members)
    peers.meet()

    for g, (first, last) in enumerate(groups):

        @pl.loop(first, last)
        def _(r):
            cells = merged(patch_ref[:, r]).astype(F32)
            mean = jnp.sum(cells, axis=0, keepdims=True) * (1.0 / members)
            result = mean + dot1(turned[...], (cells - mean).astype(BF16))
            updated[:, r] = result.reshape(patches, m, cols).astype(BF16)

        blocks.start(g)

    side = (side_send, side_recv)

    def halo(k, other):
        return beside(back.at[:, 0 if k == 0 else rows - 1], edge_in.at[1 - k], side, k, other)

    def halo_in(k, other):
        return beside(back.at[:, 0], edge_in.at[k], side, 1 - k, other)

    def take(r):
        for q in range(patches):
            xs[r + 1, :, PAD + q * cols : PAD + (q + 1) * cols] = back[q, r].astype(F32)

    def last_step(r):
        for q in range(patches):
            at = q * cols
            moved[r, :, at : at + cols] = step(
                xs, r + 1, d_ref[r, :, at : at + cols], at, cols
            ).astype(BF16)

    for k, (has, other) in enumerate(peers.sides()):
        blocks.arrive(k)
        take(0 if k == 0 else rows - 1)

        @pl.when(has)
        def _():
            halo(k, other).start()

    done = 1
    for g in range(2, len(groups)):
        first, last = groups[g]
        blocks.arrive(g)

        @pl.loop(first, last)
        def _(r):
            take(r)

        upto = last if g == len(groups) - 1 else last - 1

        @pl.loop(done, upto)
        def _(r):
            last_step(r)

        done = upto
        if g == 2:
            for k, (has, other) in enumerate(peers.sides()):
                row = 0 if k == 0 else rows + 1

                @pl.when(has)
                def _():
                    halo_in(k, other).wait_recv()
                    for q in range(patches):
                        xs[row, :, PAD + q * cols : PAD + (q + 1) * cols] = edge_in[k, q].astype(F32)

                @pl.when(jnp.logical_not(has))
                def _():
                    xs[row, :, PAD : PAD + width] = jnp.zeros((m, width), F32)

            last_step(0)
    last_step(rows - 1)

    for c in range(patches // 2):
        at = c * 2 * cols
        part = merged(moved[:, :, at : at + 2 * cols])
        out_ref[:, at : at + 2 * cols] = dot1(swap_ref[...], part).astype(BF16)
    blocks.finish()
    for k, (has, other) in enumerate(peers.sides()):

        @pl.when(has)
        def _():
            halo(k, other).wait_send()


def call(kernel, shapes, scratch, *args, name, number, flops):
    size = sum(a.size * a.dtype.itemsize for a in args)
    return pl.pallas_call(
        kernel,
        out_shape=shapes,
        in_specs=[VMEM] * len(args),
        out_specs=jax.tree.map(lambda _: VMEM, shapes),
        scratch_shapes=scratch,
        compiler_params=pltpu.CompilerParams(
            vmem_limit_bytes=50 * 2**20, collective_id=number, has_side_effects=True
        ),
        cost_estimate=pl.CostEstimate(flops=flops, bytes_accessed=size, transcendentals=0),
        name=name,
    )(*args)


def body(prior, diffusivity, site, quantities, weightings):
    m, rows, width = prior.shape
    patches = lax.axis_size("mem")
    spaces = lax.axis_size("space")
    cols = width // patches
    members = m * patches
    obs = site.shape[-1]
    padded = width + 2 * PAD
    d3 = diffusivity[:, None, :]
    dma = pltpu.SemaphoreType.DMA
    many = len(forecast_groups(rows))
    patch, own = call(
        functools.partial(forecast_kernel, spaces),
        (
            jax.ShapeDtypeStruct((patches, rows, m, cols), BF16),
            jax.ShapeDtypeStruct((members + 8, members), F32),
        ),
        [
            pltpu.VMEM((rows + 4, m, padded), F32),
            pltpu.VMEM((rows + 4, m, padded), F32),
            pltpu.VMEM((patches, rows, m, cols), BF16),
            pltpu.VMEM((2, 2, m, width), BF16),
            pltpu.VMEM((2, 2, m, width), BF16),
            pltpu.VMEM((2, 1, width), F32),
            pltpu.VMEM((members, obs), F32),
            dma((many, patches - 1)),
            dma((many, patches - 1)),
            dma((4,)),
            dma((4,)),
        ],
        prior.reshape(m * rows, width),
        swap_matrix(rows, m),
        d3,
        site[0],
        quantities[0],
        weightings[0],
        name="forecast",
        number=0,
        flops=2 * (m * rows) ** 2 * width,
    )
    sent = own.astype(BF16)
    low, high = exchange(sent, sent, "mem")
    band = own + 0.5 * (low.astype(F32) + high.astype(F32))
    sent = band.astype(BF16)
    low, high = exchange(sent, sent, "space")
    gram = band + 0.5 * (low.astype(F32) + high.astype(F32))
    many = len(analyse_groups(rows))
    out = call(
        functools.partial(analyse_kernel, spaces),
        jax.ShapeDtypeStruct((m * rows, width), BF16),
        [
            pltpu.VMEM((patches, rows, m, cols), BF16),
            pltpu.VMEM((patches, rows, m, cols), BF16),
            pltpu.VMEM((2, patches, m, cols), BF16),
            pltpu.VMEM((members, members), BF16),
            pltpu.VMEM((rows + 2, m, padded), F32),
            pltpu.VMEM((rows, m, width), BF16),
            dma((many, patches - 1)),
            dma((many, patches - 1)),
            dma((2,)),
            dma((2,)),
        ],
        gram,
        patch,
        swap_matrix(m, rows),
        d3,
        name="analyse",
        number=1,
        flops=2 * members * members * (rows * cols + 90 * members),
    )
    return out.reshape(m, rows, width)


def solution(mesh):
    return jax.shard_map(
        body,
        mesh=mesh,
        in_specs=(
            P("mem", "space", None),
            P("space", None),
            P("space", "mem", None),
            P("space", "mem", None),
            P("space", "mem", None),
        ),
        out_specs=P("mem", "space", None),
        check_vma=False,
    )
```

```python
import functools
import math

import jax
import jax.numpy as jnp
import numpy as np
from jax import lax
from jax.experimental import pallas as pl
from jax.experimental.pallas import tpu as pltpu
from jax.sharding import PartitionSpec as P

ITERS = 10
PAD = 128
F32 = jnp.float32
BF16 = jnp.bfloat16
MESH = pl.DeviceIdType.MESH
VMEM = pl.BlockSpec(memory_space=pltpu.VMEM)


def swap_matrix(outer, inner):
    row = np.arange(outer * inner)
    source = (row % inner) * outer + row // inner
    return jnp.asarray(source[:, None] == row[None, :], BF16)


def merged(block):
    a, m, c = block.shape
    if m % 16 == 0:
        return block.reshape(a * m, c)
    return block.astype(F32).reshape(a * m, c).astype(BF16)


def halves(value):
    high = value.astype(BF16)
    return high, (value - high.astype(F32)).astype(BF16)


def dot1(a, b):
    return jnp.dot(a, b, preferred_element_type=F32)


def dot3(a, b):
    ah, al = a
    bh, bl = b
    return dot1(ah, bh) + (dot1(ah, bl) + dot1(al, bh))


def step(src, row, diffusion, at, cols):
    lo = PAD + at
    mid = src[row, :, lo : lo + cols]
    around = (
        src[row - 1, :, lo : lo + cols]
        + src[row + 1, :, lo : lo + cols]
        + src[row, :, lo - 1 : lo - 1 + cols]
        + src[row, :, lo + 1 : lo + 1 + cols]
    )
    return mid + diffusion * (around - 4.0 * mid)


def clear_pads(buf, width):
    rows, m, _ = buf.shape
    buf[:, :, :PAD] = jnp.zeros((rows, m, PAD), F32)
    buf[:, :, PAD + width :] = jnp.zeros((rows, m, PAD), F32)


class Peers:
    def __init__(self, n, spaces):
        self.n = n
        self.me = lax.axis_index("mem")
        self.space = lax.axis_index("space")
        self.has_low = self.space > 0
        self.has_high = self.space < spaces - 1
        self.order = []
        for k in reversed(range(1, n)):
            peer, bit = self.me, 1
            while bit < n:
                if k & bit:
                    peer = peer + bit * (1 - 2 * ((self.me // bit) % 2))
                bit *= 2
            self.order.append(peer)

    def sides(self):
        return ((self.has_low, self.space - 1), (self.has_high, self.space + 1))

    def greet(self):
        barrier = pltpu.get_barrier_semaphore()
        for peer in self.order:
            pl.semaphore_signal(barrier, inc=1, device_id={"mem": peer}, device_id_type=MESH)
        for has, other in self.sides():

            @pl.when(has)
            def _():
                pl.semaphore_signal(barrier, inc=1, device_id={"space": other}, device_id_type=MESH)

    def meet(self):
        barrier = pltpu.get_barrier_semaphore()
        beside = self.has_low.astype(jnp.int32) + self.has_high.astype(jnp.int32)
        pl.semaphore_wait(barrier, self.n - 1 + beside)


class Blocks:
    def __init__(self, peers, src, dst, groups, send, recv):
        self.peers, self.src, self.dst = peers, src, dst
        self.groups, self.sems = groups, (send, recv)

    def copy(self, g, i, slot):
        first, last = self.groups[g]
        peer = self.peers.order[i]
        send, recv = self.sems
        return pltpu.make_async_remote_copy(
            src_ref=self.src.at[peer, first:last],
            dst_ref=self.dst.at[slot, first:last],
            send_sem=send.at[g, i],
            recv_sem=recv.at[g, i],
            device_id={"mem": peer},
            device_id_type=MESH,
        )

    def start(self, g):
        for i in range(len(self.peers.order)):
            self.copy(g, i, self.peers.me).start()
        first, last = self.groups[g]
        me = self.peers.me
        self.dst[me, first:last] = self.src[me, first:last]

    def arrive(self, g):
        for i in range(len(self.peers.order)):
            self.copy(g, i, self.peers.order[i]).wait_recv()

    def finish(self):
        for g in range(len(self.groups)):
            for i in range(len(self.peers.order)):
                self.copy(g, i, self.peers.me).wait_send()


class Rows:
    def __init__(self, peers, src, dst, send, recv):
        self.peers, self.src, self.dst = peers, src, dst
        self.send, self.recv = send, recv

    def copy(self, i, slot):
        peer = self.peers.order[i]
        return pltpu.make_async_remote_copy(
            src_ref=self.src(peer),
            dst_ref=self.dst.at[slot],
            send_sem=self.send.at[i],
            recv_sem=self.recv.at[i],
            device_id={"mem": peer},
            device_id_type=MESH,
        )

    def start(self):
        for i in range(len(self.peers.order)):
            self.copy(i, self.peers.me).start()

    def arrive(self):
        for i in range(len(self.peers.order)):
            self.copy(i, self.peers.order[i]).wait_recv()

    def finish(self):
        for i in range(len(self.peers.order)):
            self.copy(i, self.peers.me).wait_send()


def beside(src, dst, sems, slot, other):
    send, recv = sems
    return pltpu.make_async_remote_copy(
        src_ref=src,
        dst_ref=dst,
        send_sem=send.at[slot],
        recv_sem=recv.at[slot],
        device_id={"space": other},
        device_id_type=MESH,
    )


def cut(first, last, parts):
    size = -(-(last - first) // parts)
    return [(a, min(a + size, last)) for a in range(first, last, size)]


def transform_of(gram, vector, members):
    identity = (
        lax.broadcasted_iota(jnp.int32, (members, members), 0)
        == lax.broadcasted_iota(jnp.int32, (members, members), 1)
    ).astype(F32)
    system = gram + (members - 1.0) * identity
    frob = jnp.sqrt(jnp.sum(jnp.sum(system * system, axis=1, keepdims=True), axis=0, keepdims=True))
    root_part = system / frob
    factor = 1.5 * identity - 0.5 * root_part
    root_part = dot3(halves(root_part), halves(factor))
    inverse_part = factor
    for index in range(1, ITERS):
        r, z = halves(root_part), halves(inverse_part)
        f = halves(1.5 * identity - 0.5 * dot3(z, r))
        if index < ITERS - 1:
            root_part = dot3(r, f)
        inverse_part = dot3(f, z)
    inverse_root = inverse_part / jnp.sqrt(frob)
    z = halves(inverse_root)
    weights = dot3(halves(dot3(halves(vector), z)), z)[0:1, :]
    return (math.sqrt(members - 1.0) * inverse_root + weights).astype(BF16)


def row_groups(rows):
    return cut(2, rows - 2, 3), [(0, 2), (rows - 2, rows)]


def cycle_kernel(
    spaces, x_ref, swap_ref, swap_back_ref, d_ref, site_ref, value_ref, weight_ref, out_ref,
    xs, v1, fresh, patch, updated, back, moved, edge_out, edge_in, d_out, d_in, last_in,
    sites, seen_out, seen, gram_out, gram_in, turned,
    send, recv, return_send, return_recv, side_send, side_recv,
    site_send, site_recv, seen_send, seen_recv, gram_send, gram_recv,
):
    patches, rows, m, cols = patch.shape
    width = patches * cols
    members = patches * m
    obs = site_ref.shape[1]
    peers = Peers(patches, spaces)
    peers.greet()
    me = peers.me
    middle, edges = row_groups(rows)
    groups = middle[:2] + edges + middle[2:]
    blocks = Blocks(peers, fresh, patch, groups, send, recv)
    returned = edges + middle
    returns = Blocks(peers, updated, back, returned, return_send, return_recv)
    site_blocks = Rows(peers, lambda peer: sites.at[me], sites, site_send, site_recv)
    seen_blocks = Rows(peers, lambda peer: seen_out.at[peer], seen, seen_send, seen_recv)
    side = (side_send, side_recv)
    sides = list(enumerate(peers.sides()))

    sites[me] = site_ref[...]
    clear_pads(xs, width)
    clear_pads(v1, width)
    d_out[0] = d_ref[0:1, :]
    d_out[1] = d_ref[rows - 1 : rows, :]
    for c in range(patches // 2):
        at = c * 2 * cols
        part = dot1(swap_ref[...], x_ref[:, at : at + 2 * cols]).reshape(rows, m, 2 * cols)
        xs[2 : rows + 2, :, PAD + at : PAD + at + 2 * cols] = part
        edge_out[0, :, :, at : at + 2 * cols] = part[:2].astype(BF16)
        edge_out[1, :, :, at : at + 2 * cols] = part[rows - 2 :].astype(BF16)

    peers.meet()

    def halo(k, other):
        return (
            beside(edge_out.at[k], edge_in.at[1 - k], side, k, other),
            beside(d_out.at[k], d_in.at[1 - k], side, 2 + k, other),
        )

    def halo_in(k, other):
        return (
            beside(edge_out.at[k], edge_in.at[k], side, 1 - k, other),
            beside(d_out.at[k], d_in.at[k], side, 3 - k, other),
        )

    for k, (has, other) in sides:

        @pl.when(has)
        def _():
            for copy in halo(k, other):
                copy.start()

    site_blocks.start()

    def first_step(r, d_row):
        for q in range(patches):
            at = q * cols
            v1[r, :, PAD + at : PAD + at + cols] = step(xs, r, d_row(at), at, cols)

    def second_step(r):
        for q in range(patches):
            at = q * cols
            d_row = d_ref[pl.ds(r - 2, 1), at : at + cols]
            fresh[q, r - 2] = step(v1, r, d_row, at, cols).astype(BF16)

    done = 3
    for g, (first, last) in enumerate(middle):

        @pl.loop(done, last + 3)
        def _(r):
            first_step(r, lambda at: d_ref[pl.ds(r - 2, 1), at : at + cols])

        done = last + 3

        @pl.loop(first + 2, last + 2)
        def _(r):
            second_step(r)

        if g == 0:
            blocks.start(0)

    for k, (has, other) in sides:
        row = 0 if k == 0 else rows + 2

        @pl.when(has)
        def _():
            for copy in halo_in(k, other):
                copy.wait_recv()
            xs[row : row + 2, :, PAD : PAD + width] = edge_in[k].astype(F32)

        @pl.when(jnp.logical_not(has))
        def _():
            xs[row : row + 2, :, PAD : PAD + width] = jnp.zeros((2, m, width), F32)
            d_in[k] = jnp.zeros((1, width), F32)

        outer, inner = (1, 2) if k == 0 else (rows + 2, rows + 1)
        first_step(outer, lambda at: d_in[k, :, at : at + cols])
        first_step(inner, lambda at: d_ref[inner - 2 : inner - 1, at : at + cols])

        @pl.loop(edges[k][0] + 2, edges[k][1] + 2)
        def _(r):
            second_step(r)

    site_blocks.arrive()

    @pl.loop(0, patches)
    def _(q):
        lanes = 128
        at = [
            jnp.broadcast_to(sites[q, :, o * lanes : (o + 1) * lanes], (m, lanes))
            for o in range(obs // lanes)
        ]
        lane = [v % lanes for v in at]
        tile = [v // lanes for v in at]
        picked = [jnp.zeros((m, lanes), F32) for _ in at]
        for r in range(rows):
            for h in range(cols // lanes):
                cells = fresh[q, r, :, h * lanes : (h + 1) * lanes].astype(F32)
                number = r * (cols // lanes) + h
                for o in range(len(at)):
                    got = jnp.take_along_axis(cells, lane[o], axis=1, mode="promise_in_bounds")
                    picked[o] = jnp.where(tile[o] == number, got, picked[o])
        for o in range(len(at)):
            seen_out[q, :, o * lanes : (o + 1) * lanes] = picked[o].astype(BF16)

    seen_blocks.start()
    seen[me] = seen_out[me]
    blocks.start(1)
    seen_blocks.arrive()

    observed = merged(seen[...]).astype(F32)
    obs_mean = jnp.sum(observed, axis=0, keepdims=True) * (1.0 / members)
    root = jnp.sqrt(weight_ref[...])
    spread = ((observed - obs_mean) * root).astype(BF16)
    innovation = ((value_ref[...] - obs_mean) * root).astype(BF16)
    contract = (((1,), (1,)), ((), ()))
    gram_out[0, 0:members, :] = lax.dot_general(
        spread, spread, contract, preferred_element_type=F32
    )
    wide = jnp.broadcast_to(innovation.astype(F32), (8, obs)).astype(BF16)
    gram_out[0, members : members + 8, :] = lax.dot_general(
        wide, spread, contract, preferred_element_type=F32
    )

    def to_beside(stage, k, axis, other):
        return pltpu.make_async_remote_copy(
            src_ref=gram_out.at[stage],
            dst_ref=gram_in.at[stage, 1 - k],
            send_sem=gram_send.at[stage, k],
            recv_sem=gram_recv.at[stage, 1 - k],
            device_id={axis: other},
            device_id_type=MESH,
        )

    def from_beside(stage, k, axis, other):
        return pltpu.make_async_remote_copy(
            src_ref=gram_out.at[stage],
            dst_ref=gram_in.at[stage, k],
            send_sem=gram_send.at[stage, k],
            recv_sem=gram_recv.at[stage, k],
            device_id={axis: other},
            device_id_type=MESH,
        )

    def gram_send_all(stage, axis, pairs):
        for k, (has, other) in enumerate(pairs):

            @pl.when(has)
            def _():
                to_beside(stage, k, axis, other).start()

            @pl.when(jnp.logical_not(has))
            def _():
                gram_in[stage, k] = jnp.zeros((members + 8, members), F32)

    def gram_sum(stage, axis, pairs):
        for k, (has, other) in enumerate(pairs):

            @pl.when(has)
            def _():
                from_beside(stage, k, axis, other).wait_recv()

        return gram_out[stage] + 0.5 * (gram_in[stage, 0] + gram_in[stage, 1])

    along = ((me > 0, me - 1), (me < patches - 1, me + 1))
    gram_send_all(0, "mem", along)
    for g in range(2, len(groups)):
        blocks.start(g)
    gram_out[1] = gram_sum(0, "mem", along)
    gram_send_all(1, "space", peers.sides())
    gram_out[2] = gram_sum(1, "space", peers.sides())
    turned[...] = transform_of(gram_out[2, 0:members], gram_out[2, members:], members)

    arrived = set()
    for g, (first, last) in enumerate(returned):
        index = groups.index((first, last))
        for earlier in range(index + 1):
            if earlier not in arrived:
                blocks.arrive(earlier)
                arrived.add(earlier)

        @pl.loop(first, last)
        def _(r):
            cells = merged(patch[:, r]).astype(F32)
            mean = jnp.sum(cells, axis=0, keepdims=True) * (1.0 / members)
            result = mean + dot1(turned[...], (cells - mean).astype(BF16))
            updated[:, r] = result.reshape(patches, m, cols).astype(BF16)

        returns.start(g)

    def last_halo(k, other):
        row = 0 if k == 0 else rows - 1
        return beside(back.at[:, row], last_in.at[1 - k], side, 4 + k, other)

    def last_halo_in(k, other):
        return beside(back.at[:, 0], last_in.at[k], side, 5 - k, other)

    def take(r):
        for q in range(patches):
            xs[r + 1, :, PAD + q * cols : PAD + (q + 1) * cols] = back[q, r].astype(F32)

    def last_step(r, d_row):
        for q in range(patches):
            at = q * cols
            moved[r, :, at : at + cols] = step(xs, r + 1, d_row(at), at, cols).astype(BF16)

    for k, (has, other) in sides:
        returns.arrive(k)

        @pl.when(has)
        def _():
            last_halo(k, other).start()

        @pl.loop(*edges[k])
        def _(r):
            take(r)

    done = 1
    for g in range(2, len(returned)):
        first, last = returned[g]
        returns.arrive(g)

        @pl.loop(first, last)
        def _(r):
            take(r)

        upto = rows - 1 if g == len(returned) - 1 else last - 1

        @pl.loop(done, upto)
        def _(r):
            last_step(r, lambda at: d_ref[pl.ds(r, 1), at : at + cols])

        done = upto
        if g == 2:
            for k, (has, other) in sides:
                row = 0 if k == 0 else rows + 1

                @pl.when(has)
                def _():
                    last_halo_in(k, other).wait_recv()
                    for q in range(patches):
                        xs[row, :, PAD + q * cols : PAD + (q + 1) * cols] = last_in[k, q].astype(F32)

                @pl.when(jnp.logical_not(has))
                def _():
                    xs[row, :, PAD : PAD + width] = jnp.zeros((m, width), F32)

                r = 0 if k == 0 else rows - 1
                last_step(r, lambda at: d_ref[r : r + 1, at : at + cols])

    for c in range(patches // 2):
        at = c * 2 * cols
        part = merged(moved[:, :, at : at + 2 * cols])
        out_ref[:, at : at + 2 * cols] = dot1(swap_back_ref[...], part).astype(BF16)

    for sent in (blocks, returns, site_blocks, seen_blocks):
        sent.finish()
    for k, (has, other) in sides:

        @pl.when(has)
        def _():
            for copy in (*halo(k, other), last_halo(k, other)):
                copy.wait_send()

    for stage, axis, pairs in ((0, "mem", along), (1, "space", peers.sides())):
        for k, (has, other) in enumerate(pairs):

            @pl.when(has)
            def _():
                to_beside(stage, k, axis, other).wait_send()


def body(prior, diffusivity, site, quantities, weightings):
    m, rows, width = prior.shape
    patches = lax.axis_size("mem")
    spaces = lax.axis_size("space")
    cols = width // patches
    members = m * patches
    obs = site.shape[-1]
    padded = width + 2 * PAD
    dma = pltpu.SemaphoreType.DMA
    many = sum(map(len, row_groups(rows)))
    others = patches - 1
    args = (
        prior.reshape(m * rows, width),
        swap_matrix(rows, m),
        swap_matrix(m, rows),
        diffusivity,
        site[0],
        quantities[0],
        weightings[0],
    )
    bulk = pltpu.VMEM((patches, rows, m, cols), BF16)
    out = pl.pallas_call(
        functools.partial(cycle_kernel, spaces),
        out_shape=jax.ShapeDtypeStruct((m * rows, width), BF16),
        in_specs=[VMEM] * len(args),
        out_specs=VMEM,
        scratch_shapes=[
            pltpu.VMEM((rows + 4, m, padded), F32),
            pltpu.VMEM((rows + 4, m, padded), F32),
            bulk,
            bulk,
            bulk,
            bulk,
            pltpu.VMEM((rows, m, width), BF16),
            pltpu.VMEM((2, 2, m, width), BF16),
            pltpu.VMEM((2, 2, m, width), BF16),
            pltpu.VMEM((2, 1, width), F32),
            pltpu.VMEM((2, 1, width), F32),
            pltpu.VMEM((2, patches, m, cols), BF16),
            pltpu.VMEM((patches, 1, obs), jnp.int32),
            pltpu.VMEM((patches, m, obs), BF16),
            pltpu.VMEM((patches, m, obs), BF16),
            pltpu.VMEM((3, members + 8, members), F32),
            pltpu.VMEM((2, 2, members + 8, members), F32),
            pltpu.VMEM((members, members), BF16),
            *[dma((many, others))] * 4,
            dma((6,)),
            dma((6,)),
            *[dma((others,))] * 4,
            dma((2, 2)),
            dma((2, 2)),
        ],
        compiler_params=pltpu.CompilerParams(
            vmem_limit_bytes=58 * 2**20, collective_id=0, has_side_effects=True
        ),
        name="cycle",
    )(*args)
    return out.reshape(m, rows, width)


def solution(mesh):
    return jax.shard_map(
        body,
        mesh=mesh,
        in_specs=(
            P("mem", "space", None),
            P("space", None),
            P("space", "mem", None),
            P("space", "mem", None),
            P("space", "mem", None),
        ),
        out_specs=P("mem", "space", None),
        check_vma=False,
    )
```

```python
import functools
import math

import jax
import jax.numpy as jnp
import numpy as np
from jax import lax
from jax.experimental import pallas as pl
from jax.experimental.pallas import tpu as pltpu
from jax.sharding import PartitionSpec as P

ITERS = 10
PAD = 128
F32 = jnp.float32
BF16 = jnp.bfloat16
MESH = pl.DeviceIdType.MESH
VMEM = pl.BlockSpec(memory_space=pltpu.VMEM)


def swap_matrix(outer, inner):
    row = np.arange(outer * inner)
    source = (row % inner) * outer + row // inner
    return jnp.asarray(source[:, None] == row[None, :], BF16)


def merged(block):
    a, m, c = block.shape
    if m % 16 == 0:
        return block.reshape(a * m, c)
    return block.astype(F32).reshape(a * m, c).astype(BF16)


def halves(value):
    high = value.astype(BF16)
    return high, (value - high.astype(F32)).astype(BF16)


def dot1(a, b):
    return jnp.dot(a, b, preferred_element_type=F32)


def dot3(a, b):
    ah, al = a
    bh, bl = b
    return dot1(ah, bh) + (dot1(ah, bl) + dot1(al, bh))


def step(src, row, diffusion, at, cols):
    lo = PAD + at
    mid = src[row, :, lo : lo + cols]
    around = (
        src[row - 1, :, lo : lo + cols]
        + src[row + 1, :, lo : lo + cols]
        + src[row, :, lo - 1 : lo - 1 + cols]
        + src[row, :, lo + 1 : lo + 1 + cols]
    )
    return mid + diffusion * (around - 4.0 * mid)


def clear_pads(buf, width):
    rows, m, _ = buf.shape
    buf[:, :, :PAD] = jnp.zeros((rows, m, PAD), F32)
    buf[:, :, PAD + width :] = jnp.zeros((rows, m, PAD), F32)


class Peers:
    def __init__(self, n, spaces):
        self.n = n
        self.me = lax.axis_index("mem")
        self.space = lax.axis_index("space")
        self.has_low = self.space > 0
        self.has_high = self.space < spaces - 1
        self.order = []
        for k in reversed(range(1, n)):
            peer, bit = self.me, 1
            while bit < n:
                if k & bit:
                    peer = peer + bit * (1 - 2 * ((self.me // bit) % 2))
                bit *= 2
            self.order.append(peer)

    def sides(self):
        return ((self.has_low, self.space - 1), (self.has_high, self.space + 1))

    def greet(self):
        barrier = pltpu.get_barrier_semaphore()
        for peer in self.order:
            pl.semaphore_signal(barrier, inc=1, device_id={"mem": peer}, device_id_type=MESH)
        for has, other in self.sides():

            @pl.when(has)
            def _():
                pl.semaphore_signal(barrier, inc=1, device_id={"space": other}, device_id_type=MESH)

    def meet(self):
        barrier = pltpu.get_barrier_semaphore()
        beside = self.has_low.astype(jnp.int32) + self.has_high.astype(jnp.int32)
        pl.semaphore_wait(barrier, self.n - 1 + beside)


class Blocks:
    def __init__(self, peers, src, dst, groups, send, recv):
        self.peers, self.src, self.dst = peers, src, dst
        self.groups, self.sems = groups, (send, recv)

    def copy(self, g, i, slot):
        first, last = self.groups[g]
        peer = self.peers.order[i]
        send, recv = self.sems
        return pltpu.make_async_remote_copy(
            src_ref=self.src.at[peer, first:last],
            dst_ref=self.dst.at[slot, first:last],
            send_sem=send.at[g, i],
            recv_sem=recv.at[g, i],
            device_id={"mem": peer},
            device_id_type=MESH,
        )

    def start(self, g, near_first=False):
        order = range(len(self.peers.order))
        for i in reversed(order) if near_first else order:
            self.copy(g, i, self.peers.me).start()
        first, last = self.groups[g]
        me = self.peers.me
        self.dst[me, first:last] = self.src[me, first:last]

    def arrive(self, g):
        for i in range(len(self.peers.order)):
            self.copy(g, i, self.peers.order[i]).wait_recv()

    def finish(self):
        for g in range(len(self.groups)):
            for i in range(len(self.peers.order)):
                self.copy(g, i, self.peers.me).wait_send()


class Rows:
    def __init__(self, peers, src, dst, send, recv):
        self.peers, self.src, self.dst = peers, src, dst
        self.send, self.recv = send, recv

    def copy(self, i, slot):
        peer = self.peers.order[i]
        return pltpu.make_async_remote_copy(
            src_ref=self.src(peer),
            dst_ref=self.dst.at[slot],
            send_sem=self.send.at[i],
            recv_sem=self.recv.at[i],
            device_id={"mem": peer},
            device_id_type=MESH,
        )

    def start(self):
        for i in range(len(self.peers.order)):
            self.copy(i, self.peers.me).start()

    def arrive(self):
        for i in range(len(self.peers.order)):
            self.copy(i, self.peers.order[i]).wait_recv()

    def finish(self):
        for i in range(len(self.peers.order)):
            self.copy(i, self.peers.me).wait_send()


def beside(src, dst, sems, slot, other):
    send, recv = sems
    return pltpu.make_async_remote_copy(
        src_ref=src,
        dst_ref=dst,
        send_sem=send.at[slot],
        recv_sem=recv.at[slot],
        device_id={"space": other},
        device_id_type=MESH,
    )


def cut(first, last, parts):
    size = -(-(last - first) // parts)
    return [(a, min(a + size, last)) for a in range(first, last, size)]


def transform_of(gram, vector, members):
    identity = (
        lax.broadcasted_iota(jnp.int32, (members, members), 0)
        == lax.broadcasted_iota(jnp.int32, (members, members), 1)
    ).astype(F32)
    system = gram + (members - 1.0) * identity
    frob = jnp.sqrt(jnp.sum(jnp.sum(system * system, axis=1, keepdims=True), axis=0, keepdims=True))
    root_part = system / frob
    factor = 1.5 * identity - 0.5 * root_part
    root_part = dot3(halves(root_part), halves(factor))
    inverse_part = factor
    for index in range(1, ITERS):
        r, z = halves(root_part), halves(inverse_part)
        f = halves(1.5 * identity - 0.5 * dot3(z, r))
        if index < ITERS - 1:
            root_part = dot3(r, f)
        inverse_part = dot3(f, z)
    inverse_root = inverse_part / jnp.sqrt(frob)
    z = halves(inverse_root)
    weights = dot3(halves(dot3(halves(vector), z)), z)[0:1, :]
    return (math.sqrt(members - 1.0) * inverse_root + weights).astype(BF16)


def row_groups(rows):
    return cut(2, rows - 2, 3), [(0, 2), (rows - 2, rows)]


def swap_kernel(swap_ref, moved_ref, out_ref):
    out_ref[...] = dot1(swap_ref[...], merged(moved_ref[...])).astype(BF16)


def return_groups(rows):
    middle, edges = row_groups(rows)
    return edges + middle[:-1] + cut(*middle[-1], 2)


def cycle_kernel(
    spaces, x_ref, swap_ref, d_ref, site_ref, value_ref, weight_ref, moved,
    xs, v1, fresh, patch, updated, back, edge_out, edge_in, d_out, d_in, last_in,
    sites, seen_out, seen, gram_out, gram_in, turned,
    send, recv, return_send, return_recv, side_send, side_recv,
    site_send, site_recv, seen_send, seen_recv, gram_send, gram_recv,
):
    patches, rows, m, cols = patch.shape
    width = patches * cols
    members = patches * m
    obs = site_ref.shape[1]
    peers = Peers(patches, spaces)
    peers.greet()
    me = peers.me
    middle, edges = row_groups(rows)
    groups = middle[:2] + edges + middle[2:]
    blocks = Blocks(peers, fresh, patch, groups, send, recv)
    returned = return_groups(rows)
    returns = Blocks(peers, updated, back, returned, return_send, return_recv)
    site_blocks = Rows(peers, lambda peer: sites.at[me], sites, site_send, site_recv)
    seen_blocks = Rows(peers, lambda peer: seen_out.at[peer], seen, seen_send, seen_recv)
    side = (side_send, side_recv)
    sides = list(enumerate(peers.sides()))

    sites[me] = site_ref[...]
    clear_pads(xs, width)
    clear_pads(v1, width)
    d_out[0] = d_ref[0:1, :]
    d_out[1] = d_ref[rows - 1 : rows, :]
    for c in range(patches // 2):
        at = c * 2 * cols
        part = dot1(swap_ref[...], x_ref[:, at : at + 2 * cols]).reshape(rows, m, 2 * cols)
        xs[2 : rows + 2, :, PAD + at : PAD + at + 2 * cols] = part
        edge_out[0, :, :, at : at + 2 * cols] = part[:2].astype(BF16)
        edge_out[1, :, :, at : at + 2 * cols] = part[rows - 2 :].astype(BF16)

    peers.meet()

    def halo(k, other):
        return (
            beside(edge_out.at[k], edge_in.at[1 - k], side, k, other),
            beside(d_out.at[k], d_in.at[1 - k], side, 2 + k, other),
        )

    def halo_in(k, other):
        return (
            beside(edge_out.at[k], edge_in.at[k], side, 1 - k, other),
            beside(d_out.at[k], d_in.at[k], side, 3 - k, other),
        )

    for k, (has, other) in sides:

        @pl.when(has)
        def _():
            for copy in halo(k, other):
                copy.start()

    site_blocks.start()

    def first_step(r, d_row):
        for q in range(patches):
            at = q * cols
            v1[r, :, PAD + at : PAD + at + cols] = step(xs, r, d_row(at), at, cols)

    def second_step(r):
        for q in range(patches):
            at = q * cols
            d_row = d_ref[pl.ds(r - 2, 1), at : at + cols]
            fresh[q, r - 2] = step(v1, r, d_row, at, cols).astype(BF16)

    done = 3
    for g, (first, last) in enumerate(middle):

        @pl.loop(done, last + 3)
        def _(r):
            first_step(r, lambda at: d_ref[pl.ds(r - 2, 1), at : at + cols])

        done = last + 3

        @pl.loop(first + 2, last + 2)
        def _(r):
            second_step(r)

        if g == 0:
            blocks.start(0)

    for k, (has, other) in sides:
        row = 0 if k == 0 else rows + 2

        @pl.when(has)
        def _():
            for copy in halo_in(k, other):
                copy.wait_recv()
            xs[row : row + 2, :, PAD : PAD + width] = edge_in[k].astype(F32)

        @pl.when(jnp.logical_not(has))
        def _():
            xs[row : row + 2, :, PAD : PAD + width] = jnp.zeros((2, m, width), F32)
            d_in[k] = jnp.zeros((1, width), F32)

        outer, inner = (1, 2) if k == 0 else (rows + 2, rows + 1)
        first_step(outer, lambda at: d_in[k, :, at : at + cols])
        first_step(inner, lambda at: d_ref[inner - 2 : inner - 1, at : at + cols])

        @pl.loop(edges[k][0] + 2, edges[k][1] + 2)
        def _(r):
            second_step(r)

    site_blocks.arrive()

    @pl.loop(0, patches)
    def _(q):
        lanes = 128
        at = [
            jnp.broadcast_to(sites[q, :, o * lanes : (o + 1) * lanes], (m, lanes))
            for o in range(obs // lanes)
        ]
        lane = [v % lanes for v in at]
        tile = [v // lanes for v in at]
        picked = [jnp.zeros((m, lanes), F32) for _ in at]
        for r in range(rows):
            for h in range(cols // lanes):
                cells = fresh[q, r, :, h * lanes : (h + 1) * lanes].astype(F32)
                number = r * (cols // lanes) + h
                for o in range(len(at)):
                    got = jnp.take_along_axis(cells, lane[o], axis=1, mode="promise_in_bounds")
                    picked[o] = jnp.where(tile[o] == number, got, picked[o])
        for o in range(len(at)):
            seen_out[q, :, o * lanes : (o + 1) * lanes] = picked[o].astype(BF16)

    seen_blocks.start()
    seen[me] = seen_out[me]
    blocks.start(1)
    seen_blocks.arrive()

    observed = merged(seen[...]).astype(F32)
    obs_mean = jnp.sum(observed, axis=0, keepdims=True) * (1.0 / members)
    root = jnp.sqrt(weight_ref[...])
    spread = ((observed - obs_mean) * root).astype(BF16)
    innovation = ((value_ref[...] - obs_mean) * root).astype(BF16)
    contract = (((1,), (1,)), ((), ()))
    gram_out[0, 0:members, :] = lax.dot_general(
        spread, spread, contract, preferred_element_type=F32
    )
    wide = jnp.broadcast_to(innovation.astype(F32), (8, obs)).astype(BF16)
    gram_out[0, members : members + 8, :] = lax.dot_general(
        wide, spread, contract, preferred_element_type=F32
    )

    def to_beside(stage, k, axis, other):
        return pltpu.make_async_remote_copy(
            src_ref=gram_out.at[stage],
            dst_ref=gram_in.at[stage, 1 - k],
            send_sem=gram_send.at[stage, k],
            recv_sem=gram_recv.at[stage, 1 - k],
            device_id={axis: other},
            device_id_type=MESH,
        )

    def from_beside(stage, k, axis, other):
        return pltpu.make_async_remote_copy(
            src_ref=gram_out.at[stage],
            dst_ref=gram_in.at[stage, k],
            send_sem=gram_send.at[stage, k],
            recv_sem=gram_recv.at[stage, k],
            device_id={axis: other},
            device_id_type=MESH,
        )

    def gram_send_all(stage, axis, pairs):
        for k, (has, other) in enumerate(pairs):

            @pl.when(has)
            def _():
                to_beside(stage, k, axis, other).start()

            @pl.when(jnp.logical_not(has))
            def _():
                gram_in[stage, k] = jnp.zeros((members + 8, members), F32)

    def gram_sum(stage, axis, pairs):
        for k, (has, other) in enumerate(pairs):

            @pl.when(has)
            def _():
                from_beside(stage, k, axis, other).wait_recv()

        return gram_out[stage] + 0.5 * (gram_in[stage, 0] + gram_in[stage, 1])

    along = ((me > 0, me - 1), (me < patches - 1, me + 1))
    gram_send_all(0, "mem", along)
    for g in range(2, len(groups)):
        blocks.start(g)
    gram_out[1] = gram_sum(0, "mem", along)
    gram_send_all(1, "space", peers.sides())
    gram_out[2] = gram_sum(1, "space", peers.sides())
    turned[...] = transform_of(gram_out[2, 0:members], gram_out[2, members:], members)

    arrived = set()
    for g, (first, last) in enumerate(returned):
        index = max(i for i, (low, high) in enumerate(groups) if low < last and high > first)
        for earlier in range(index + 1):
            if earlier not in arrived:
                blocks.arrive(earlier)
                arrived.add(earlier)

        @pl.loop(first, last)
        def _(r):
            cells = merged(patch[:, r]).astype(F32)
            mean = jnp.sum(cells, axis=0, keepdims=True) * (1.0 / members)
            result = mean + dot1(turned[...], (cells - mean).astype(BF16))
            updated[:, r] = result.reshape(patches, m, cols).astype(BF16)

        returns.start(g, near_first=g == len(returned) - 1)

    def last_halo(k, other):
        row = 0 if k == 0 else rows - 1
        return beside(back.at[:, row], last_in.at[1 - k], side, 4 + k, other)

    def last_halo_in(k, other):
        return beside(back.at[:, 0], last_in.at[k], side, 5 - k, other)

    def take(r):
        for q in range(patches):
            xs[r + 1, :, PAD + q * cols : PAD + (q + 1) * cols] = back[q, r].astype(F32)

    def last_step(r, d_row):
        for q in range(patches):
            at = q * cols
            moved[r, :, at : at + cols] = step(xs, r + 1, d_row(at), at, cols).astype(BF16)

    for k, (has, other) in sides:
        returns.arrive(k)

        @pl.when(has)
        def _():
            last_halo(k, other).start()

        @pl.loop(*edges[k])
        def _(r):
            take(r)

    done = 1
    for g in range(2, len(returned)):
        first, last = returned[g]
        returns.arrive(g)

        @pl.loop(first, last)
        def _(r):
            take(r)

        upto = rows - 1 if g == len(returned) - 1 else last - 1

        @pl.loop(done, upto)
        def _(r):
            last_step(r, lambda at: d_ref[pl.ds(r, 1), at : at + cols])

        done = upto
        if g == 2:
            for k, (has, other) in sides:
                row = 0 if k == 0 else rows + 1

                @pl.when(has)
                def _():
                    last_halo_in(k, other).wait_recv()
                    for q in range(patches):
                        xs[row, :, PAD + q * cols : PAD + (q + 1) * cols] = last_in[k, q].astype(F32)

                @pl.when(jnp.logical_not(has))
                def _():
                    xs[row, :, PAD : PAD + width] = jnp.zeros((m, width), F32)

                r = 0 if k == 0 else rows - 1
                last_step(r, lambda at: d_ref[r : r + 1, at : at + cols])

    for sent in (blocks, returns, site_blocks, seen_blocks):
        sent.finish()
    for k, (has, other) in sides:

        @pl.when(has)
        def _():
            for copy in (*halo(k, other), last_halo(k, other)):
                copy.wait_send()

    for stage, axis, pairs in ((0, "mem", along), (1, "space", peers.sides())):
        for k, (has, other) in enumerate(pairs):

            @pl.when(has)
            def _():
                to_beside(stage, k, axis, other).wait_send()


def body(prior, diffusivity, site, quantities, weightings):
    m, rows, width = prior.shape
    patches = lax.axis_size("mem")
    spaces = lax.axis_size("space")
    cols = width // patches
    members = m * patches
    obs = site.shape[-1]
    padded = width + 2 * PAD
    dma = pltpu.SemaphoreType.DMA
    many = sum(map(len, row_groups(rows)))
    others = patches - 1
    args = (
        prior.reshape(m * rows, width),
        swap_matrix(rows, m),
        diffusivity,
        site[0],
        quantities[0],
        weightings[0],
    )
    bulk = pltpu.VMEM((patches, rows, m, cols), BF16)
    moved = pl.pallas_call(
        functools.partial(cycle_kernel, spaces),
        out_shape=jax.ShapeDtypeStruct((rows, m, width), BF16),
        in_specs=[VMEM] * len(args),
        out_specs=VMEM,
        scratch_shapes=[
            pltpu.VMEM((rows + 4, m, padded), F32),
            pltpu.VMEM((rows + 4, m, padded), F32),
            bulk,
            bulk,
            bulk,
            bulk,
            pltpu.VMEM((2, 2, m, width), BF16),
            pltpu.VMEM((2, 2, m, width), BF16),
            pltpu.VMEM((2, 1, width), F32),
            pltpu.VMEM((2, 1, width), F32),
            pltpu.VMEM((2, patches, m, cols), BF16),
            pltpu.VMEM((patches, 1, obs), jnp.int32),
            pltpu.VMEM((patches, m, obs), BF16),
            pltpu.VMEM((patches, m, obs), BF16),
            pltpu.VMEM((3, members + 8, members), F32),
            pltpu.VMEM((2, 2, members + 8, members), F32),
            pltpu.VMEM((members, members), BF16),
            *[dma((many, others))] * 2,
            *[dma((len(return_groups(rows)), others))] * 2,
            dma((6,)),
            dma((6,)),
            *[dma((others,))] * 4,
            dma((2, 2)),
            dma((2, 2)),
        ],
        compiler_params=pltpu.CompilerParams(
            vmem_limit_bytes=58 * 2**20, collective_id=0, has_side_effects=True
        ),
        name="cycle",
    )(*args)
    size, lanes = m * rows, width // 4
    out = pl.pallas_call(
        swap_kernel,
        out_shape=jax.ShapeDtypeStruct((size, width), BF16),
        grid=(4,),
        in_specs=[
            pl.BlockSpec((size, size), lambda c: (0, 0)),
            pl.BlockSpec((rows, m, lanes), lambda c: (0, 0, c)),
        ],
        out_specs=pl.BlockSpec((size, lanes), lambda c: (0, c)),
        name="swap",
    )(swap_matrix(m, rows), moved)
    return out.reshape(m, rows, width)


def solution(mesh):
    return jax.shard_map(
        body,
        mesh=mesh,
        in_specs=(
            P("mem", "space", None),
            P("space", None),
            P("space", "mem", None),
            P("space", "mem", None),
            P("space", "mem", None),
        ),
        out_specs=P("mem", "space", None),
        check_vma=False,
    )
```

```python
import functools
import math

import jax
import jax.numpy as jnp
import numpy as np
from jax import lax
from jax.experimental import pallas as pl
from jax.experimental.pallas import tpu as pltpu
from jax.sharding import PartitionSpec as P

ITERS = 10
PAD = 128
F32 = jnp.float32
BF16 = jnp.bfloat16
MESH = pl.DeviceIdType.MESH
VMEM = pl.BlockSpec(memory_space=pltpu.VMEM)


def swap_matrix(outer, inner):
    row = np.arange(outer * inner)
    source = (row % inner) * outer + row // inner
    return jnp.asarray(source[:, None] == row[None, :], BF16)


def merged(block):
    a, m, c = block.shape
    if m % 16 == 0:
        return block.reshape(a * m, c)
    return block.astype(F32).reshape(a * m, c).astype(BF16)


def halves(value):
    high = value.astype(BF16)
    return high, (value - high.astype(F32)).astype(BF16)


def dot1(a, b):
    return jnp.dot(a, b, preferred_element_type=F32)


def dot3(a, b):
    ah, al = a
    bh, bl = b
    return dot1(ah, bh) + (dot1(ah, bl) + dot1(al, bh))


def step(src, row, diffusion, at, cols):
    lo = PAD + at
    mid = src[row, :, lo : lo + cols]
    around = (
        src[row - 1, :, lo : lo + cols]
        + src[row + 1, :, lo : lo + cols]
        + src[row, :, lo - 1 : lo - 1 + cols]
        + src[row, :, lo + 1 : lo + 1 + cols]
    )
    return mid + diffusion * (around - 4.0 * mid)


def clear_pads(buf, width):
    rows, m, _ = buf.shape
    buf[:, :, :PAD] = jnp.zeros((rows, m, PAD), F32)
    buf[:, :, PAD + width :] = jnp.zeros((rows, m, PAD), F32)


class Peers:
    def __init__(self, n, spaces):
        self.n = n
        self.me = lax.axis_index("mem")
        self.space = lax.axis_index("space")
        self.has_low = self.space > 0
        self.has_high = self.space < spaces - 1
        self.order = []
        for k in reversed(range(1, n)):
            peer, bit = self.me, 1
            while bit < n:
                if k & bit:
                    peer = peer + bit * (1 - 2 * ((self.me // bit) % 2))
                bit *= 2
            self.order.append(peer)

    def sides(self):
        return ((self.has_low, self.space - 1), (self.has_high, self.space + 1))

    def greet(self):
        barrier = pltpu.get_barrier_semaphore()
        for peer in self.order:
            pl.semaphore_signal(barrier, inc=1, device_id={"mem": peer}, device_id_type=MESH)
        for has, other in self.sides():

            @pl.when(has)
            def _():
                pl.semaphore_signal(barrier, inc=1, device_id={"space": other}, device_id_type=MESH)

    def meet(self):
        barrier = pltpu.get_barrier_semaphore()
        beside = self.has_low.astype(jnp.int32) + self.has_high.astype(jnp.int32)
        pl.semaphore_wait(barrier, self.n - 1 + beside)


class Blocks:
    def __init__(self, peers, src, dst, groups, send, recv):
        self.peers, self.src, self.dst = peers, src, dst
        self.groups, self.sems = groups, (send, recv)

    def copy(self, g, i, slot):
        first, last = self.groups[g]
        peer = self.peers.order[i]
        send, recv = self.sems
        return pltpu.make_async_remote_copy(
            src_ref=self.src.at[peer, first:last],
            dst_ref=self.dst.at[slot, first:last],
            send_sem=send.at[g, i],
            recv_sem=recv.at[g, i],
            device_id={"mem": peer},
            device_id_type=MESH,
        )

    def start(self, g, near_first=False):
        order = range(len(self.peers.order))
        for i in reversed(order) if near_first else order:
            self.copy(g, i, self.peers.me).start()
        first, last = self.groups[g]
        me = self.peers.me
        self.dst[me, first:last] = self.src[me, first:last]

    def arrive(self, g):
        for i in range(len(self.peers.order)):
            self.copy(g, i, self.peers.order[i]).wait_recv()

    def finish(self):
        for g in range(len(self.groups)):
            for i in range(len(self.peers.order)):
                self.copy(g, i, self.peers.me).wait_send()


class Rows:
    def __init__(self, peers, src, dst, send, recv):
        self.peers, self.src, self.dst = peers, src, dst
        self.send, self.recv = send, recv

    def copy(self, i, slot):
        peer = self.peers.order[i]
        return pltpu.make_async_remote_copy(
            src_ref=self.src(peer),
            dst_ref=self.dst.at[slot],
            send_sem=self.send.at[i],
            recv_sem=self.recv.at[i],
            device_id={"mem": peer},
            device_id_type=MESH,
        )

    def start(self):
        for i in range(len(self.peers.order)):
            self.copy(i, self.peers.me).start()

    def arrive(self):
        for i in range(len(self.peers.order)):
            self.copy(i, self.peers.order[i]).wait_recv()

    def finish(self):
        for i in range(len(self.peers.order)):
            self.copy(i, self.peers.me).wait_send()


def beside(src, dst, sems, slot, other):
    send, recv = sems
    return pltpu.make_async_remote_copy(
        src_ref=src,
        dst_ref=dst,
        send_sem=send.at[slot],
        recv_sem=recv.at[slot],
        device_id={"space": other},
        device_id_type=MESH,
    )


def cut(first, last, parts):
    size = -(-(last - first) // parts)
    return [(a, min(a + size, last)) for a in range(first, last, size)]


def transform_of(gram, vector, members):
    identity = (
        lax.broadcasted_iota(jnp.int32, (members, members), 0)
        == lax.broadcasted_iota(jnp.int32, (members, members), 1)
    ).astype(F32)
    system = gram + (members - 1.0) * identity
    frob = jnp.sqrt(jnp.sum(jnp.sum(system * system, axis=1, keepdims=True), axis=0, keepdims=True))
    root_part = system / frob
    factor = 1.5 * identity - 0.5 * root_part
    root_part = dot3(halves(root_part), halves(factor))
    inverse_part = factor
    for index in range(1, ITERS):
        r, z = halves(root_part), halves(inverse_part)
        f = halves(1.5 * identity - 0.5 * dot3(z, r))
        if index < ITERS - 1:
            root_part = dot3(r, f)
        inverse_part = dot3(f, z)
    inverse_root = inverse_part / jnp.sqrt(frob)
    z = halves(inverse_root)
    weights = dot3(halves(dot3(halves(vector), z)), z)[0:1, :]
    return (math.sqrt(members - 1.0) * inverse_root + weights).astype(BF16)


def row_groups(rows):
    return cut(2, rows - 2, 4), [(0, 2), (rows - 2, rows)]


def swap_kernel(swap_ref, moved_ref, out_ref):
    out_ref[...] = dot1(swap_ref[...], merged(moved_ref[...])).astype(BF16)


def return_groups(rows):
    middle, edges = row_groups(rows)
    return edges + middle[:-1] + cut(*middle[-1], 2)


def cycle_kernel(
    spaces, x_ref, swap_ref, d_ref, site_ref, value_ref, weight_ref, moved,
    xs, v1, fresh, patch, updated, back, edge_out, edge_in, d_out, d_in, last_in,
    sites, seen_out, seen, gram_out, gram_in, turned,
    send, recv, return_send, return_recv, side_send, side_recv,
    site_send, site_recv, seen_send, seen_recv, gram_send, gram_recv,
):
    patches, rows, m, cols = patch.shape
    width = patches * cols
    members = patches * m
    obs = site_ref.shape[1]
    peers = Peers(patches, spaces)
    peers.greet()
    me = peers.me
    middle, edges = row_groups(rows)
    groups = middle[:3] + edges + middle[3:]
    blocks = Blocks(peers, fresh, patch, groups, send, recv)
    returned = return_groups(rows)
    returns = Blocks(peers, updated, back, returned, return_send, return_recv)
    site_blocks = Rows(peers, lambda peer: sites.at[me], sites, site_send, site_recv)
    seen_blocks = Rows(peers, lambda peer: seen_out.at[peer], seen, seen_send, seen_recv)
    side = (side_send, side_recv)
    sides = list(enumerate(peers.sides()))

    sites[me] = site_ref[...]
    clear_pads(xs, width)
    clear_pads(v1, width)
    d_out[0] = d_ref[0:1, :]
    d_out[1] = d_ref[rows - 1 : rows, :]
    for c in range(patches // 2):
        at = c * 2 * cols
        part = dot1(swap_ref[...], x_ref[:, at : at + 2 * cols]).reshape(rows, m, 2 * cols)
        xs[2 : rows + 2, :, PAD + at : PAD + at + 2 * cols] = part
        edge_out[0, :, :, at : at + 2 * cols] = part[:2].astype(BF16)
        edge_out[1, :, :, at : at + 2 * cols] = part[rows - 2 :].astype(BF16)

    peers.meet()

    def halo(k, other):
        return (
            beside(edge_out.at[k], edge_in.at[1 - k], side, k, other),
            beside(d_out.at[k], d_in.at[1 - k], side, 2 + k, other),
        )

    def halo_in(k, other):
        return (
            beside(edge_out.at[k], edge_in.at[k], side, 1 - k, other),
            beside(d_out.at[k], d_in.at[k], side, 3 - k, other),
        )

    for k, (has, other) in sides:

        @pl.when(has)
        def _():
            for copy in halo(k, other):
                copy.start()

    site_blocks.start()

    def first_step(r, d_row):
        for q in range(patches):
            at = q * cols
            v1[r, :, PAD + at : PAD + at + cols] = step(xs, r, d_row(at), at, cols)

    def second_step(r):
        for q in range(patches):
            at = q * cols
            d_row = d_ref[pl.ds(r - 2, 1), at : at + cols]
            fresh[q, r - 2] = step(v1, r, d_row, at, cols).astype(BF16)

    done = 3
    for g, (first, last) in enumerate(middle):

        @pl.loop(done, last + 3)
        def _(r):
            first_step(r, lambda at: d_ref[pl.ds(r - 2, 1), at : at + cols])

        done = last + 3

        @pl.loop(first + 2, last + 2)
        def _(r):
            second_step(r)

        if g < 2:
            blocks.start(g)

    for k, (has, other) in sides:
        row = 0 if k == 0 else rows + 2

        @pl.when(has)
        def _():
            for copy in halo_in(k, other):
                copy.wait_recv()
            xs[row : row + 2, :, PAD : PAD + width] = edge_in[k].astype(F32)

        @pl.when(jnp.logical_not(has))
        def _():
            xs[row : row + 2, :, PAD : PAD + width] = jnp.zeros((2, m, width), F32)
            d_in[k] = jnp.zeros((1, width), F32)

        outer, inner = (1, 2) if k == 0 else (rows + 2, rows + 1)
        first_step(outer, lambda at: d_in[k, :, at : at + cols])
        first_step(inner, lambda at: d_ref[inner - 2 : inner - 1, at : at + cols])

        @pl.loop(edges[k][0] + 2, edges[k][1] + 2)
        def _(r):
            second_step(r)

    site_blocks.arrive()

    @pl.loop(0, patches)
    def _(q):
        lanes = 128
        at = [
            jnp.broadcast_to(sites[q, :, o * lanes : (o + 1) * lanes], (m, lanes))
            for o in range(obs // lanes)
        ]
        lane = [v % lanes for v in at]
        tile = [v // lanes for v in at]
        picked = [jnp.zeros((m, lanes), F32) for _ in at]
        for r in range(rows):
            for h in range(cols // lanes):
                cells = fresh[q, r, :, h * lanes : (h + 1) * lanes].astype(F32)
                number = r * (cols // lanes) + h
                for o in range(len(at)):
                    got = jnp.take_along_axis(cells, lane[o], axis=1, mode="promise_in_bounds")
                    picked[o] = jnp.where(tile[o] == number, got, picked[o])
        for o in range(len(at)):
            seen_out[q, :, o * lanes : (o + 1) * lanes] = picked[o].astype(BF16)

    seen_blocks.start()
    seen[me] = seen_out[me]
    blocks.start(2)
    seen_blocks.arrive()

    observed = merged(seen[...]).astype(F32)
    obs_mean = jnp.sum(observed, axis=0, keepdims=True) * (1.0 / members)
    root = jnp.sqrt(weight_ref[...])
    spread = ((observed - obs_mean) * root).astype(BF16)
    innovation = ((value_ref[...] - obs_mean) * root).astype(BF16)
    contract = (((1,), (1,)), ((), ()))
    gram_out[0, 0:members, :] = lax.dot_general(
        spread, spread, contract, preferred_element_type=F32
    )
    wide = jnp.broadcast_to(innovation.astype(F32), (8, obs)).astype(BF16)
    gram_out[0, members : members + 8, :] = lax.dot_general(
        wide, spread, contract, preferred_element_type=F32
    )

    def to_beside(stage, k, axis, other):
        return pltpu.make_async_remote_copy(
            src_ref=gram_out.at[stage],
            dst_ref=gram_in.at[stage, 1 - k],
            send_sem=gram_send.at[stage, k],
            recv_sem=gram_recv.at[stage, 1 - k],
            device_id={axis: other},
            device_id_type=MESH,
        )

    def from_beside(stage, k, axis, other):
        return pltpu.make_async_remote_copy(
            src_ref=gram_out.at[stage],
            dst_ref=gram_in.at[stage, k],
            send_sem=gram_send.at[stage, k],
            recv_sem=gram_recv.at[stage, k],
            device_id={axis: other},
            device_id_type=MESH,
        )

    def gram_send_all(stage, axis, pairs):
        for k, (has, other) in enumerate(pairs):

            @pl.when(has)
            def _():
                to_beside(stage, k, axis, other).start()

            @pl.when(jnp.logical_not(has))
            def _():
                gram_in[stage, k] = jnp.zeros((members + 8, members), F32)

    def gram_sum(stage, axis, pairs):
        for k, (has, other) in enumerate(pairs):

            @pl.when(has)
            def _():
                from_beside(stage, k, axis, other).wait_recv()

        return gram_out[stage] + 0.5 * (gram_in[stage, 0] + gram_in[stage, 1])

    along = ((me > 0, me - 1), (me < patches - 1, me + 1))
    gram_send_all(0, "mem", along)
    for g in range(3, len(groups)):
        blocks.start(g)
    gram_out[1] = gram_sum(0, "mem", along)
    gram_send_all(1, "space", peers.sides())
    gram_out[2] = gram_sum(1, "space", peers.sides())
    turned[...] = transform_of(gram_out[2, 0:members], gram_out[2, members:], members)

    arrived = set()
    for g, (first, last) in enumerate(returned):
        index = max(i for i, (low, high) in enumerate(groups) if low < last and high > first)
        for earlier in range(index + 1):
            if earlier not in arrived:
                blocks.arrive(earlier)
                arrived.add(earlier)

        @pl.loop(first, last)
        def _(r):
            cells = merged(patch[:, r]).astype(F32)
            mean = jnp.sum(cells, axis=0, keepdims=True) * (1.0 / members)
            result = mean + dot1(turned[...], (cells - mean).astype(BF16))
            updated[:, r] = result.reshape(patches, m, cols).astype(BF16)

        returns.start(g, near_first=g == len(returned) - 1)

    def last_halo(k, other):
        row = 0 if k == 0 else rows - 1
        return beside(back.at[:, row], last_in.at[1 - k], side, 4 + k, other)

    def last_halo_in(k, other):
        return beside(back.at[:, 0], last_in.at[k], side, 5 - k, other)

    def take(r):
        for q in range(patches):
            xs[r + 1, :, PAD + q * cols : PAD + (q + 1) * cols] = back[q, r].astype(F32)

    def last_step(r, d_row):
        for q in range(patches):
            at = q * cols
            moved[r, :, at : at + cols] = step(xs, r + 1, d_row(at), at, cols).astype(BF16)

    for k, (has, other) in sides:
        returns.arrive(k)

        @pl.when(has)
        def _():
            last_halo(k, other).start()

        @pl.loop(*edges[k])
        def _(r):
            take(r)

    done = 1
    for g in range(2, len(returned)):
        first, last = returned[g]
        returns.arrive(g)

        @pl.loop(first, last)
        def _(r):
            take(r)

        upto = rows - 1 if g == len(returned) - 1 else last - 1

        @pl.loop(done, upto)
        def _(r):
            last_step(r, lambda at: d_ref[pl.ds(r, 1), at : at + cols])

        done = upto
        if g == 2:
            for k, (has, other) in sides:
                row = 0 if k == 0 else rows + 1

                @pl.when(has)
                def _():
                    last_halo_in(k, other).wait_recv()
                    for q in range(patches):
                        xs[row, :, PAD + q * cols : PAD + (q + 1) * cols] = last_in[k, q].astype(F32)

                @pl.when(jnp.logical_not(has))
                def _():
                    xs[row, :, PAD : PAD + width] = jnp.zeros((m, width), F32)

                r = 0 if k == 0 else rows - 1
                last_step(r, lambda at: d_ref[r : r + 1, at : at + cols])

    for sent in (blocks, returns, site_blocks, seen_blocks):
        sent.finish()
    for k, (has, other) in sides:

        @pl.when(has)
        def _():
            for copy in (*halo(k, other), last_halo(k, other)):
                copy.wait_send()

    for stage, axis, pairs in ((0, "mem", along), (1, "space", peers.sides())):
        for k, (has, other) in enumerate(pairs):

            @pl.when(has)
            def _():
                to_beside(stage, k, axis, other).wait_send()


def body(prior, diffusivity, site, quantities, weightings):
    m, rows, width = prior.shape
    patches = lax.axis_size("mem")
    spaces = lax.axis_size("space")
    cols = width // patches
    members = m * patches
    obs = site.shape[-1]
    padded = width + 2 * PAD
    dma = pltpu.SemaphoreType.DMA
    many = sum(map(len, row_groups(rows)))
    others = patches - 1
    args = (
        prior.reshape(m * rows, width),
        swap_matrix(rows, m),
        diffusivity,
        site[0],
        quantities[0],
        weightings[0],
    )
    bulk = pltpu.VMEM((patches, rows, m, cols), BF16)
    moved = pl.pallas_call(
        functools.partial(cycle_kernel, spaces),
        out_shape=jax.ShapeDtypeStruct((rows, m, width), BF16),
        in_specs=[VMEM] * len(args),
        out_specs=VMEM,
        scratch_shapes=[
            pltpu.VMEM((rows + 4, m, padded), F32),
            pltpu.VMEM((rows + 4, m, padded), F32),
            bulk,
            bulk,
            bulk,
            bulk,
            pltpu.VMEM((2, 2, m, width), BF16),
            pltpu.VMEM((2, 2, m, width), BF16),
            pltpu.VMEM((2, 1, width), F32),
            pltpu.VMEM((2, 1, width), F32),
            pltpu.VMEM((2, patches, m, cols), BF16),
            pltpu.VMEM((patches, 1, obs), jnp.int32),
            pltpu.VMEM((patches, m, obs), BF16),
            pltpu.VMEM((patches, m, obs), BF16),
            pltpu.VMEM((3, members + 8, members), F32),
            pltpu.VMEM((2, 2, members + 8, members), F32),
            pltpu.VMEM((members, members), BF16),
            *[dma((many, others))] * 2,
            *[dma((len(return_groups(rows)), others))] * 2,
            dma((6,)),
            dma((6,)),
            *[dma((others,))] * 4,
            dma((2, 2)),
            dma((2, 2)),
        ],
        compiler_params=pltpu.CompilerParams(
            vmem_limit_bytes=36 * 2**20, collective_id=0, has_side_effects=True
        ),
        name="cycle",
    )(*args)
    size, lanes = m * rows, width // 4
    out = pl.pallas_call(
        swap_kernel,
        out_shape=jax.ShapeDtypeStruct((size, width), BF16),
        grid=(4,),
        in_specs=[
            pl.BlockSpec((size, size), lambda c: (0, 0)),
            pl.BlockSpec((rows, m, lanes), lambda c: (0, 0, c)),
        ],
        out_specs=pl.BlockSpec((size, lanes), lambda c: (0, c)),
        compiler_params=pltpu.CompilerParams(vmem_limit_bytes=16 * 2**20),
        name="swap",
    )(swap_matrix(m, rows), moved)
    return out.reshape(m, rows, width)


def solution(mesh):
    return jax.shard_map(
        body,
        mesh=mesh,
        in_specs=(
            P("mem", "space", None),
            P("space", None),
            P("space", "mem", None),
            P("space", "mem", None),
            P("space", "mem", None),
        ),
        out_specs=P("mem", "space", None),
        check_vma=False,
    )
```
